256 devices in a mesh: bank: 64 (over x_hi, z, y), tp: 4 (over x_lo, core).
Axes of the slice: x: 4 (x_hi: 2, x_lo: 2; x = x_hi * 2 + x_lo), y: 4, z: 8, core: 2. Of those that a mesh axis runs over, the one named last changes fastest.
Arguments:
- hidden: bfloat16 [128, 512, 14336], P('bank', None, 'tp'), may hold values from -6 to 6
- out_grad: bfloat16 [128, 512, 4096], P('bank', None, 'tp'), may hold values from -6 to 6
- proj_in: bfloat16 [64, 14336], P(None, 'tp'), may hold values from -0.046875 to 0.046875
- proj_out: bfloat16 [64, 4096], P(None, 'tp'), may hold values from -0.09375 to 0.09375
- lengths: int32 [128], P('bank'), may hold values from 1 to 512, 49152 in all
- pair_perm: int32 [128], replicated, may hold values from 0 to 127, each once
- bank_slab: bfloat16 [65536, 4096], P('bank', 'tp'), may hold values from -6 to 6
Outputs:
- scores: float32 [64, 65536], P('tp', 'bank')
The draws below stay inside these ranges and needn't reach their ends.
Inputs may be any that keep to these rules, and one draw needn't show every extreme that they name: pair_perm holds every variant index exactly once. `lengths`: some prompt fills all 512 slots.
All inputs are finite; a program needn't handle non-finite values. No bound on the sum of `lengths` on one device may be relied on, other than what follows from the above.
Results may differ from the reference program's by a relative error of at most 0.0029.
Values sent between devices are 32-bit elements; how exact they have to be, the bound alone decides.
A program may use at most 64 MiB of HBM per device.

```python
import math
import jax
import jax.numpy as jnp
import numpy as np
from jax import lax

D = 4096
FF = 14336
RANK = 64
SEQ = 512
EXAMPLES = 128
BANK_ROWS = 65536


def level_of(own_key, extent, split, least, largest):
    level = 1.0
    for position, parts in split:
        heights = jax.random.uniform(jax.random.fold_in(jax.random.fold_in(own_key, 6), position), (parts,), jnp.float32, least / len(split), largest / len(split))
        level = level * jnp.repeat(jnp.exp(heights), extent[position] // parts).reshape((-1,) + (1,) * (len(extent) - 1 - position))
    return level


def length_profile(amount, total, limit, skew):
    loads = [(1 << 20) // math.isqrt(rank ** skew) + 1 for rank in range(2, amount + 1)]
    surplus, counts = total - limit - (amount - 1), [1] * (amount - 1)
    while surplus > 0:
        candidates = [i for i in range(amount - 1) if counts[i] < limit]
        whole, remaining = sum([loads[i] for i in candidates]), surplus
        for i in candidates:
            more = min(limit - counts[i], max(1, remaining * loads[i] // whole), surplus)
            counts[i] = counts[i] + more
            surplus = surplus - more
    return np.array([limit] + counts)


def uneven(stream_key, count, total, reach, skew):
    if count == 2:
        one = jax.random.randint(stream_key, (), max(1, total - reach), min(reach, total - 1) + 1)
        return jnp.stack([one, total - one])
    sizes = jnp.asarray(length_profile(count, total, reach, skew), jnp.int32)
    couples = (count - 1) // 2
    donor, sink = sizes[1:1 + 2 * couples:2], sizes[2:2 + 2 * couples:2]
    room = jnp.minimum(donor - 1, reach - sink)
    moved = jax.random.randint(jax.random.fold_in(stream_key, 1), (couples,), 0, 1 << 20) % (room + 1)
    sizes = sizes.at[1:1 + 2 * couples:2].set(donor - moved).at[2:2 + 2 * couples:2].set(sink + moved)
    return sizes[jax.random.permutation(jax.random.fold_in(stream_key, 2), count)]


def noise(key, dims, scale, reach, pieces=(), held_as=jnp.bfloat16):
    level = level_of(key, dims, pieces, -0.22, 0.18) if pieces else 1.0
    values = jax.random.normal(key, dims, jnp.float32) * scale * level
    return jnp.minimum(jnp.maximum(values, -reach), reach).astype(held_as)


def setup_inputs(seed: int = 0) -> dict:
    key_of = jax.random.split(jax.random.key(seed), 8)
    return {
        "hidden": noise(key_of[0], (EXAMPLES, SEQ, FF), 1.0, 6.0, ((0, 64), (2, 4))),
        "out_grad": noise(key_of[1], (EXAMPLES, SEQ, D), 1.0, 6.0, ((0, 64), (2, 4))),
        "proj_in": noise(key_of[2], (RANK, FF), FF ** -0.5, 0.046875, ((1, 4),)),
        "proj_out": noise(key_of[3], (RANK, D), D ** -0.5, 0.09375, ((1, 4),)),
        "lengths": uneven(key_of[4], EXAMPLES, EXAMPLES * (SEQ // 2 + SEQ // 4), SEQ, 0).astype(jnp.int32),
        "pair_perm": jax.random.permutation(key_of[5], EXAMPLES).astype(jnp.int32),
        "bank_slab": noise(key_of[6], (BANK_ROWS, RANK * RANK), 1.0, 6.0, ((0, 64), (1, 4))),
    }


epsilon = 1e-06

def reference(hidden, out_grad, proj_in, proj_out, lengths, pair_perm, bank_slab):
    positions = jnp.arange(SEQ, dtype=jnp.int32)

    def one_example(packed):
        hid_rows, grad_rows, length_one = packed
        in_factor = jnp.dot(hid_rows, proj_in.T, preferred_element_type=jnp.float32)
        out_factor = jnp.dot(grad_rows, proj_out.T, preferred_element_type=jnp.float32)
        live_mask = (positions < length_one).astype(jnp.float32)
        masked = in_factor * live_mask[:, None]
        outer = jnp.dot(masked.T, out_factor, precision=lax.Precision.HIGHEST)
        return outer.reshape(RANK * RANK)
    grads = lax.map(one_example, (hidden, out_grad, lengths))
    benign = pair_perm[0::2]
    harmful = pair_perm[1::2]
    queries = grads[harmful] - grads[benign]
    query_sq = lax.optimization_barrier(jnp.sum(queries * queries, axis=1))
    slab_wide = bank_slab.astype(jnp.float32)
    bank_sq = lax.optimization_barrier(jnp.sum(slab_wide * slab_wide, axis=1))
    query_low = queries.astype(jnp.bfloat16)
    dots = lax.dot_general(query_low, bank_slab, (((1,), (1,)), ((), ())), preferred_element_type=jnp.float32)
    return dots * RANK * lax.rsqrt(query_sq + epsilon)[:, None] * lax.rsqrt(bank_sq + epsilon)[None, :]
```

```python
import jax
import jax.numpy as jnp
from jax import lax
from jax.experimental import pallas as pl
from jax.experimental.pallas import tpu as pltpu
from jax.sharding import PartitionSpec as P

EPS = 1e-06
MESH = pl.DeviceIdType.MESH
F32, BF16 = jnp.float32, jnp.bfloat16
NX, NY, NZ = 4, 4, 8
TOK = 256
HI = lax.Precision.HIGHEST
NT = (((1,), (1,)), ((), ()))
ORDER = (0, 1, 7, 2, 6, 3, 5, 4)
FAR = (4, 3, 5, 2, 6, 1, 7, 0)
LAG = 3


def kernel(
    len_hbm, perm_hbm, hid, og, pin, pout, bank, out_ref,
    len_s, perm_s, slot_s, win, wout, hbuf, obuf, bbuf, xbuf, xsend, r1, r2, r3,
    gsc, tbuf, r4, tsum, gb, qf, qsb, qr, dbuf, dr, btile, br, sqb,
    ld_sem, h_sem, o_sem, x_ss, x_rs, g_ss, g_rs, ys_ss, ys_rs, yr_ss, yr_rs,
    b_ss, b_rs, q_ss, q_rs, d_ss, d_rs,
):
    b, k = lax.axis_index("bank"), lax.axis_index("tp")
    xh, z, y = b // (NZ * NY), (b // NY) % NZ, b % NY
    xl, c = k // 2, k % 2
    x = xh * 2 + xl

    def dev(xx, yy, zz, cc):
        return ((xx // 2) * (NZ * NY) + zz * NY + yy, (xx % 2) * 2 + cc)

    tp_of = {1: xl * 2 + 1 - c, 2: (1 - xl) * 2 + c, 3: (1 - xl) * 2 + 1 - c}

    owners = ((1 - xl, 1 - c), (1 - xl, c), (xl, 1 - c), (xl, c))
    loads = []

    def load(src, dst, sem):
        cp = pltpu.make_async_copy(src, dst, sem)
        cp.start()
        return cp

    cp_pout = load(pout, wout.at[pl.ds(64, 64)], ld_sem.at[1])
    cp_pin = load(pin, win.at[pl.ds(0, 64)], ld_sem.at[0])
    for s, (xo, co) in enumerate(owners):
        rows = pl.ds(pl.multiple_of(co * TOK, TOK), TOK)
        loads.append(
            (
                load(og.at[xo, rows], obuf.at[s], o_sem.at[s]),
                load(hid.at[xo, rows], hbuf.at[s], h_sem.at[s]),
            )
        )
    cp_len = load(len_hbm, len_s, ld_sem.at[2])
    cp_perm = load(perm_hbm, perm_s, ld_sem.at[3])
    cp_bank = load(bank, bbuf, ld_sem.at[4])

    barrier = pltpu.get_barrier_semaphore()
    peers = []
    for dz in range(NZ):
        for dx in range(NX):
            if dx or dz:
                peers.append(dev((x + dx) % NX, y, (z + dz) % NZ, c))
    peers.append(dev(x, (y + 1) % NY, z, c))
    peers.append(dev(x, (y + NY - 1) % NY, z, c))
    peers.append((b, tp_of[1]))
    peers.append((b, tp_of[3]))
    for peer in peers:
        pl.semaphore_signal(barrier, inc=1, device_id=peer, device_id_type=MESH)

    win[pl.ds(64, 64), :] = jnp.zeros((64, win.shape[1]), BF16)
    wout[pl.ds(0, 64), :] = jnp.zeros((64, wout.shape[1]), BF16)
    cp_pout.wait()
    cp_pin.wait()

    def send(src, dst, ss, rs, to):
        cp = pltpu.make_async_remote_copy(
            src_ref=src, dst_ref=dst, send_sem=ss, recv_sem=rs, device_id=to, device_id_type=MESH
        )
        cp.start()
        return cp

    sent = []

    def factors(s):
        loads[s][0].wait()
        loads[s][1].wait()
        part = lax.dot_general(obuf[s], wout[...], NT, preferred_element_type=F32)
        return part + lax.dot_general(hbuf[s], win[...], NT, preferred_element_type=F32)

    xbuf[0] = factors(0)
    pl.semaphore_wait(barrier, len(peers))
    c1 = send(xbuf.at[0], r1, x_ss.at[0], x_rs.at[0], (b, tp_of[1]))
    xbuf[1] = factors(1)
    c1.wait_recv()
    xsend[...] = xbuf[1] + r1[...]
    c2 = send(xsend, r2, x_ss.at[1], x_rs.at[1], (b, tp_of[2]))
    xbuf[2] = factors(2)
    c3 = send(xbuf.at[2], r3, x_ss.at[2], x_rs.at[2], (b, tp_of[1]))
    own = factors(3)
    cp_len.wait()
    cp_perm.wait()
    c3.wait_recv()
    own = own + r3[...]
    c2.wait_recv()
    own = own + r2[...]
    sent += [c1, c2, c3]

    pos = lax.broadcasted_iota(jnp.int32, (TOK, 128), 0) + c * TOK
    lane = lax.broadcasted_iota(jnp.int32, (TOK, 128), 1)
    live = jnp.where(pos < len_s[xl], own, 0.0)
    twice = jnp.where(lane < 64, pltpu.roll(own, 64, axis=1), own)
    gsc[...] = jnp.dot(jnp.transpose(live)[0:64], twice, precision=HI, preferred_element_type=F32)
    even, odd = gsc[pl.ds(0, 32, stride=2), :], gsc[pl.ds(1, 32, stride=2), :]
    tiles = jnp.where(lane[0:32] < 64, even, odd)
    for to_x in range(2):
        for to_c in range(2):
            share = to_x * 2 + to_c
            tbuf[to_c, to_x] = tiles[8 * share : 8 * share + 8]
    c4 = send(tbuf.at[1 - c], r4, x_ss.at[3], x_rs.at[3], (b, tp_of[1]))
    c4.wait_recv()
    sent.append(c4)
    tsum[...] = tbuf[c] + r4[...]
    mine = y * (NZ * NX) + z * NX + x
    gb[mine] = tsum[xl]

    plane = {}
    for dz in FAR:
        for dx in (2, 1, 3, 0):
            if dx or dz:
                tx, tz = (x + dx) % NX, (z + dz) % NZ
                plane[dx, dz] = send(
                    tsum.at[tx % 2], gb.at[mine], g_ss.at[dz * NX + dx], g_rs.at[dz * NX + dx], dev(tx, y, tz, c)
                )
    sent += list(plane.values())

    cp_bank.wait()

    def bank_rows(i, carry):
        rows = pl.ds(pl.multiple_of(i * 128, 128), 128)
        acc = jnp.zeros((128, 128), F32)
        for j in range(8):
            v = bbuf[rows, pl.ds(128 * j, 128)].astype(F32)
            acc = acc + v * v
        sqb[rows, :] = acc
        return carry

    lax.fori_loop(0, 8, bank_rows, 0)
    sums = lax.dot_general(jnp.ones((8, 128), F32), sqb[...], NT, precision=HI, preferred_element_type=F32)
    sub = lax.broadcasted_iota(jnp.int32, (8, 128), 0)
    tile = jnp.zeros((8, 128), F32)
    for j in range(8):
        tile = jnp.where(sub == j, sums[:, 128 * j : 128 * j + 128], tile)
    btile[...] = tile
    bcp = {r: send(btile, br.at[r - 1], b_ss.at[r - 1], b_rs.at[r - 1], (b, tp_of[r])) for r in (1, 2, 3)}

    def slots(i, carry):
        e = perm_s[i]
        slot_s[i] = ((e // 2) % 4) * (NZ * NX) + ((e // 8) % 8) * NX + (e // 64) * 2 + e % 2
        return carry

    lax.fori_loop(0, 128, slots, 0)

    up, down = dev(x, (y + 1) % NY, z, c), dev(x, (y + NY - 1) % NY, z, c)

    def group(yy, dz):
        return gb.at[pl.ds(((yy + NY) % NY) * (NZ * NX) + ((z - dz + NZ) % NZ) * NX, NX)]

    near_up, near_down, far = {}, {}, {}

    def relay(dz):
        i = ORDER.index(dz)
        if i % 2 == 0:
            near_up[dz].wait_recv()
            far[dz] = send(group(y - 1, dz), group(y - 1, dz), yr_ss.at[dz], yr_rs.at[dz], up)
        else:
            near_down[dz].wait_recv()
            far[dz] = send(group(y + 1, dz), group(y + 1, dz), yr_ss.at[dz], yr_rs.at[dz], down)

    for i, dz in enumerate(ORDER):
        for dx in range(NX):
            if dx or dz:
                plane[dx, dz].wait_recv()
        near_up[dz] = send(group(y, dz), group(y, dz), ys_ss.at[dz], ys_rs.at[dz], up)
        near_down[dz] = send(group(y, dz), group(y, dz), ys_ss.at[8 + dz], ys_rs.at[8 + dz], down)
        if i >= LAG:
            relay(ORDER[i - LAG])
    for dz in ORDER[len(ORDER) - LAG :]:
        relay(dz)
    for i, dz in enumerate(ORDER):
        (near_down if i % 2 == 0 else near_up)[dz].wait_recv()
    for dz in ORDER:
        far[dz].wait_recv()
    sent += list(near_up.values()) + list(near_down.values()) + list(far.values())

    def query(p, carry):
        rows = pl.ds(pl.multiple_of(p * 8, 8), 8)
        qf[rows, :] = gb[slot_s[2 * p + 1]] - gb[slot_s[2 * p]]
        return carry

    lax.fori_loop(0, 64, query, 0, unroll=8)
    cols, acc = [], jnp.zeros((64, 128), F32)
    for v in range(8):
        part = qf[pl.ds(v, 64, stride=8), :]
        acc = acc + part * part
        cols.append(part.astype(BF16))
    low = jnp.concatenate(cols, axis=1)
    qsq = jnp.broadcast_to(jnp.sum(acc, axis=1, keepdims=True), (64, 128))
    for s in range(4):
        qsb[s] = qsq[16 * s : 16 * s + 16]
    qcp = {r: send(qsb.at[tp_of[r]], qr.at[r - 1], q_ss.at[r - 1], q_rs.at[r - 1], (b, tp_of[r])) for r in (2, 3, 1)}
    dcp = {}
    for j in range(4):
        part = lax.dot_general(low, bbuf[pl.ds(256 * j, 256), :], NT, preferred_element_type=F32)
        for s in range(4):
            dbuf[j, s] = part[16 * s : 16 * s + 16]
        for r in (2, 3, 1):
            dcp[j, r] = send(
                dbuf.at[j, tp_of[r]], dr.at[j, r - 1], d_ss.at[j * 3 + r - 1], d_rs.at[j * 3 + r - 1], (b, tp_of[r])
            )
    for r in (1, 2, 3):
        bcp[r].wait_recv()
    norms = lax.rsqrt(btile[...] + br[0] + br[1] + br[2] + EPS)
    for r in (1, 2, 3):
        qcp[r].wait_recv()
    scale = lax.rsqrt(qsb[k] + qr[0] + qr[1] + qr[2] + EPS) * 64.0
    for j in range(4):
        for r in (1, 2, 3):
            dcp[j, r].wait_recv()
        for h in range(2):
            cs = pl.ds(128 * h, 128)
            total = dbuf[j, k, :, cs] + dr[j, 0, :, cs] + dr[j, 1, :, cs] + dr[j, 2, :, cs]
            n = 2 * j + h
            out_ref[:, pl.ds(128 * n, 128)] = total * scale * norms[n : n + 1, :]
    sent += list(bcp.values()) + list(qcp.values()) + list(dcp.values())
    for cp in sent:
        cp.wait_send()


def per_device(hidden, out_grad, proj_in, proj_out, lengths, pair_perm, bank_slab):
    ff, d = hidden.shape[2], out_grad.shape[2]
    any_spec = pl.BlockSpec(memory_space=pl.ANY)
    V, D = pltpu.VMEM, pltpu.SemaphoreType.DMA
    return pl.pallas_call(
        kernel,
        out_shape=jax.ShapeDtypeStruct((16, 1024), F32),
        in_specs=[any_spec] * 7,
        out_specs=pl.BlockSpec(memory_space=pltpu.VMEM),
        scratch_shapes=[
            pltpu.SMEM((2,), jnp.int32),
            pltpu.SMEM((128,), jnp.int32),
            pltpu.SMEM((128,), jnp.int32),
            V((128, ff), BF16),
            V((128, d), BF16),
            V((4, TOK, ff), BF16),
            V((4, TOK, d), BF16),
            V((1024, 1024), BF16),
            V((3, TOK, 128), F32),
            V((TOK, 128), F32),
            V((TOK, 128), F32),
            V((TOK, 128), F32),
            V((TOK, 128), F32),
            V((64, 128), F32),
            V((2, 2, 8, 128), F32),
            V((2, 8, 128), F32),
            V((2, 8, 128), F32),
            V((128, 8, 128), F32),
            V((512, 128), F32),
            V((4, 16, 128), F32),
            V((3, 16, 128), F32),
            V((4, 4, 16, 256), F32),
            V((4, 3, 16, 256), F32),
            V((8, 128), F32),
            V((3, 8, 128), F32),
            V((1024, 128), F32),
            D((5,)),
            D((4,)),
            D((4,)),
            D((4,)),
            D((4,)),
            D((32,)),
            D((32,)),
            D((16,)),
            D((16,)),
            D((8,)),
            D((8,)),
            D((3,)),
            D((3,)),
            D((3,)),
            D((3,)),
            D((12,)),
            D((12,)),
        ],
        compiler_params=pltpu.CompilerParams(
            collective_id=0, has_side_effects=True, vmem_limit_bytes=60 * 1024 * 1024
        ),
    )(lengths, pair_perm, hidden, out_grad, proj_in, proj_out, bank_slab)


def solution(mesh):
    return jax.shard_map(
        per_device,
        mesh=mesh,
        in_specs=(
            P("bank", None, "tp"),
            P("bank", None, "tp"),
            P(None, "tp"),
            P(None, "tp"),
            P("bank"),
            P(),
            P("bank", "tp"),
        ),
        out_specs=P("tp", "bank"),
        check_vma=False,
    )
```

```python
import jax
import jax.numpy as jnp
from jax import lax
from jax.experimental import pallas as pl
from jax.experimental.pallas import tpu as pltpu
from jax.sharding import PartitionSpec as P

EPS = 1e-06
MESH = pl.DeviceIdType.MESH
F32, BF16 = jnp.float32, jnp.bfloat16
NX, NY, NZ = 4, 4, 8
TOK = 256
HI = lax.Precision.HIGHEST
NT = (((1,), (1,)), ((), ()))
EARLY, LATE = (0, 1, 2, 3), (7, 4, 6, 5)
GROUPS = (0, 1, 2, 3, 7, 6, 5, 4)


def kernel(
    len_hbm, perm_hbm, hid, og, pin, pout, bank, out_ref,
    len_s, perm_s, slot_s, win, wout, hbuf, obuf, bbuf, part, total, ra, rc, rx,
    gsc, tbuf, r4, tsum, gb, qf, qsb, qr, dbuf, dr, btile, br, sqb,
    ld_sem, h_sem, o_sem, x_ss, x_rs, g_ss, g_rs, y_ss, y_rs, ready,
    b_ss, b_rs, q_ss, q_rs, d_ss, d_rs,
):
    b, k = lax.axis_index("bank"), lax.axis_index("tp")
    xh, z, y = b // (NZ * NY), (b // NY) % NZ, b % NY
    xl, c = k // 2, k % 2
    x = xh * 2 + xl

    def dev(xx, yy, zz, cc):
        return ((xx // 2) * (NZ * NY) + zz * NY + yy, (xx % 2) * 2 + cc)

    tp_of = {1: xl * 2 + 1 - c, 2: (1 - xl) * 2 + c, 3: (1 - xl) * 2 + 1 - c}

    owners = ((1 - xl, c), (1 - xl, 1 - c), (xl, 1 - c), (xl, c))

    def load(src, dst, sem):
        cp = pltpu.make_async_copy(src, dst, sem)
        cp.start()
        return cp

    def block(s):
        xo, co = owners[s]
        return xo, pl.ds(pl.multiple_of(co * TOK, TOK), TOK)

    def load_og(s):
        return load(og.at[block(s)], obuf.at[s], o_sem.at[s])

    def load_hid(s):
        return load(hid.at[block(s)], hbuf.at[s], h_sem.at[s])

    cp_pout = load(pout, wout.at[0, pl.ds(0, 64)], ld_sem.at[1])
    ogs = [load_og(0), load_og(1)]
    cp_pin = load(pin, win.at[0, pl.ds(0, 64)], ld_sem.at[0])
    hids = [load_hid(0)]

    barrier = pltpu.get_barrier_semaphore()

    def greet(sem, to):
        pl.semaphore_signal(sem, inc=1, device_id=to, device_id_type=MESH)

    for r in (1, 2, 3):
        greet(barrier, (b, tp_of[r]))
    for zz in range(NZ):
        for xx in range(NX):

            @pl.when(jnp.logical_or(zz > z, jnp.logical_and(zz == z, xx // 2 > xh)))
            def _(zz=zz, xx=xx):
                greet(barrier, dev(xx, y, zz, c))

    for yy in range(1, NY):

        @pl.when(yy > y)
        def _(yy=yy):
            greet(barrier, dev(x, yy, z, c))

    def greet_back():
        for zz in range(NZ):

            @pl.when(jnp.logical_and(xh == 1, jnp.logical_or(zz < z, jnp.logical_and(zz == z, xl == 0))))
            def _(zz=zz):
                for dx in range(2):
                    greet(ready.at[z], dev(2 * xl + dx, y, zz, c))

        for yy in range(NY - 1):

            @pl.when(yy < y)
            def _(yy=yy):
                greet(ready.at[NZ], dev(x, yy, z, c))

    for w in (win, wout):
        w[0, pl.ds(64, 64)] = jnp.zeros((64, w.shape[2]), BF16)
        w[1, pl.ds(0, 64)] = jnp.zeros((64, w.shape[2]), BF16)

    def send(src, dst, ss, rs, to):
        cp = pltpu.make_async_remote_copy(
            src_ref=src, dst_ref=dst, send_sem=ss, recv_sem=rs, device_id=to, device_id_type=MESH
        )
        cp.start()
        return cp

    sent = []

    def packed(rows, s, w):
        low = lax.dot_general(rows[s, pl.ds(0, 128)], w[0], NT, preferred_element_type=F32)
        return low + lax.dot_general(rows[s, pl.ds(128, 128)], w[1], NT, preferred_element_type=F32)

    pair, cross = (b, tp_of[1]), (b, tp_of[3])
    cp_pout.wait()
    wout[1, pl.ds(64, 64)] = wout[0, pl.ds(0, 64)]
    ogs[0].wait()
    hids.append(load_hid(1))
    part[0, 0] = packed(obuf, 0, wout)
    pl.semaphore_wait(barrier, 3 + NX * z + 2 * xh + y)
    greet_back()
    ca = [send(part.at[0, 0], ra.at[0], x_ss.at[0], x_rs.at[0], pair)]
    ogs[1].wait()
    out_b = packed(obuf, 1, wout)
    cp_pin.wait()
    win[1, pl.ds(64, 64)] = win[0, pl.ds(0, 64)]
    hids[0].wait()
    ogs += [load_og(2), load_og(3)]
    hids.append(load_hid(2))
    part[0, 1] = packed(hbuf, 0, win)
    ca.append(send(part.at[0, 1], ra.at[1], x_ss.at[1], x_rs.at[1], pair))
    ca[0].wait_recv()
    total[0] = out_b + ra[0]
    cx = [send(total.at[0], rx.at[0], x_ss.at[2], x_rs.at[2], cross)]
    hids[1].wait()
    hids.append(load_hid(3))
    in_b = packed(hbuf, 1, win)
    ca[1].wait_recv()
    total[1] = in_b + ra[1]
    cx.append(send(total.at[1], rx.at[1], x_ss.at[3], x_rs.at[3], cross))
    cp_len = load(len_hbm, len_s, ld_sem.at[2])
    cp_perm = load(perm_hbm, perm_s, ld_sem.at[3])
    cp_bank = load(bank, bbuf, ld_sem.at[4])
    ogs[2].wait()
    part[1, 0] = packed(obuf, 2, wout)
    cc = [send(part.at[1, 0], rc.at[0], x_ss.at[4], x_rs.at[4], pair)]
    hids[2].wait()
    part[1, 1] = packed(hbuf, 2, win)
    cc.append(send(part.at[1, 1], rc.at[1], x_ss.at[5], x_rs.at[5], pair))
    ogs[3].wait()
    out_d = packed(obuf, 3, wout)
    hids[3].wait()
    in_d = packed(hbuf, 3, win)
    cp_len.wait()
    cp_perm.wait()
    cc[0].wait_recv()
    cx[0].wait_recv()
    out_d = out_d + rc[0] + rx[0]
    cc[1].wait_recv()
    in_d = in_d + rc[1]
    cx[1].wait_recv()
    in_d = in_d + rx[1]
    sent += ca + cx + cc

    lane = lax.broadcasted_iota(jnp.int32, (128, 128), 1)
    pos = lax.broadcasted_iota(jnp.int32, (128, 128), 0) + jnp.where(lane < 64, 0, 128) + c * TOK
    live = jnp.where(pos < len_s[xl], in_d, 0.0)
    outer = jnp.dot(jnp.transpose(live), out_d, precision=HI, preferred_element_type=F32)
    halves = jnp.where(lane[0:64] < 64, outer[0:64], outer[64:128])
    gsc[...] = halves + pltpu.roll(halves, 64, axis=1)
    even, odd = gsc[pl.ds(0, 32, stride=2), :], gsc[pl.ds(1, 32, stride=2), :]
    tiles = jnp.where(lane[0:32] < 64, even, odd)
    for to_x in range(2):
        for to_c in range(2):
            share = to_x * 2 + to_c
            tbuf[to_c, to_x] = tiles[8 * share : 8 * share + 8]
    c4 = send(tbuf.at[1 - c], r4, x_ss.at[6], x_rs.at[6], pair)
    c4.wait_recv()
    sent.append(c4)
    tsum[...] = tbuf[c] + r4[...]
    mine = y * (NZ * NX) + z * NX + x
    gb[mine] = tsum[xl]

    def plane_copy(tx, tz, slot):
        return pltpu.make_async_remote_copy(
            src_ref=tsum.at[tx % 2], dst_ref=gb.at[mine], send_sem=g_ss.at[slot], recv_sem=g_rs.at[z * NX + x],
            device_id=dev(tx, y, tz, c), device_id_type=MESH,
        )

    def to_rows(rows):
        for tz in rows:

            @pl.when(jnp.logical_or(tz > z, jnp.logical_and(tz == z, xh == 0)))
            def _(tz=tz):
                pl.semaphore_wait(ready.at[tz], 1)

            for dx in (2, 1, 3):
                plane_copy((x + dx) % NX, tz, tz * NX + dx).start()

            @pl.when(tz != z)
            def _(tz=tz):
                plane_copy(x, tz, tz * NX).start()

    to_rows(EARLY)

    @pl.when(z >= 4)
    def _():
        to_rows(LATE)

    cp_bank.wait()

    def bank_rows(i, carry):
        rows = pl.ds(pl.multiple_of(i * 128, 128), 128)
        acc = jnp.zeros((128, 128), F32)
        for j in range(8):
            v = bbuf[rows, pl.ds(128 * j, 128)].astype(F32)
            acc = acc + v * v
        sqb[rows, :] = acc
        return carry

    lax.fori_loop(0, 8, bank_rows, 0)
    sums = lax.dot_general(jnp.ones((8, 128), F32), sqb[...], NT, precision=HI, preferred_element_type=F32)
    sub = lax.broadcasted_iota(jnp.int32, (8, 128), 0)
    tile = jnp.zeros((8, 128), F32)
    for j in range(8):
        tile = jnp.where(sub == j, sums[:, 128 * j : 128 * j + 128], tile)
    btile[...] = tile
    bcp = {r: send(btile, br.at[r - 1], b_ss.at[r - 1], b_rs.at[r - 1], (b, tp_of[r])) for r in (1, 2, 3)}

    def slots(i, carry):
        e = perm_s[i]
        slot_s[i] = ((e // 2) % 4) * (NZ * NX) + ((e // 8) % 8) * NX + (e // 64) * 2 + e % 2
        return carry

    lax.fori_loop(0, 128, slots, 0)

    up, down = dev(x, (y + 1) % NY, z, c), dev(x, (y + NY - 1) % NY, z, c)

    def group(yy, zz):
        return gb.at[pl.ds(((yy + NY) % NY) * (NZ * NX) + zz * NX, NX)]

    def plane_wait(zz, xx):
        pltpu.make_async_remote_copy(
            src_ref=tsum.at[0], dst_ref=gb.at[mine], send_sem=g_ss.at[0], recv_sem=g_rs.at[zz * NX + xx],
            device_id=up, device_id_type=MESH,
        ).wait_recv()

    across = dev(x, (y + 2) % NY, z, c)
    along = []

    @pl.when(y < NY - 1)
    def _():
        pl.semaphore_wait(ready.at[NZ], NY - 1 - y)

    for i, zz in enumerate(GROUPS):
        if i == 1:

            @pl.when(z < 4)
            def _():
                to_rows(LATE)

        for xx in range(NX):

            @pl.when(jnp.logical_or(zz != z, xx != x))
            def _(zz=zz, xx=xx):
                plane_wait(zz, xx)

        for n, to in enumerate((across, up, down)):
            slot = n * NZ + zz
            along.append(send(group(y, zz), group(y, zz), y_ss.at[slot], y_rs.at[slot], to))
    for cp in along:
        cp.wait_recv()
    sent += along

    def query(p, carry):
        rows = pl.ds(pl.multiple_of(p * 8, 8), 8)
        qf[rows, :] = gb[slot_s[2 * p + 1]] - gb[slot_s[2 * p]]
        return carry

    lax.fori_loop(0, 64, query, 0, unroll=8)
    cols, acc = [], jnp.zeros((64, 128), F32)
    for v in range(8):
        part = qf[pl.ds(v, 64, stride=8), :]
        acc = acc + part * part
        cols.append(part.astype(BF16))
    low = jnp.concatenate(cols, axis=1)
    qsq = jnp.broadcast_to(jnp.sum(acc, axis=1, keepdims=True), (64, 128))
    for s in range(4):
        qsb[s] = qsq[16 * s : 16 * s + 16]
    qcp = {r: send(qsb.at[tp_of[r]], qr.at[r - 1], q_ss.at[r - 1], q_rs.at[r - 1], (b, tp_of[r])) for r in (2, 3, 1)}
    dcp = {}
    for j in range(4):
        part = lax.dot_general(low, bbuf[pl.ds(256 * j, 256), :], NT, preferred_element_type=F32)
        for s in range(4):
            dbuf[j, s] = part[16 * s : 16 * s + 16]
        for r in (2, 3, 1):
            dcp[j, r] = send(
                dbuf.at[j, tp_of[r]], dr.at[j, r - 1], d_ss.at[j * 3 + r - 1], d_rs.at[j * 3 + r - 1], (b, tp_of[r])
            )
    for r in (1, 2, 3):
        bcp[r].wait_recv()
    norms = lax.rsqrt(btile[...] + br[0] + br[1] + br[2] + EPS)
    for r in (1, 2, 3):
        qcp[r].wait_recv()
    scale = lax.rsqrt(qsb[k] + qr[0] + qr[1] + qr[2] + EPS) * 64.0
    for j in range(4):
        for r in (1, 2, 3):
            dcp[j, r].wait_recv()
        for h in range(2):
            cs = pl.ds(128 * h, 128)
            total = dbuf[j, k, :, cs] + dr[j, 0, :, cs] + dr[j, 1, :, cs] + dr[j, 2, :, cs]
            n = 2 * j + h
            out_ref[:, pl.ds(128 * n, 128)] = total * scale * norms[n : n + 1, :]
    sent += list(bcp.values()) + list(qcp.values()) + list(dcp.values())
    for cp in sent:
        cp.wait_send()
    for tz in EARLY + LATE:
        for dx in (2, 1, 3):
            plane_copy((x + dx) % NX, tz, tz * NX + dx).wait_send()

        @pl.when(tz != z)
        def _(tz=tz):
            plane_copy(x, tz, tz * NX).wait_send()


def per_device(hidden, out_grad, proj_in, proj_out, lengths, pair_perm, bank_slab):
    ff, d = hidden.shape[2], out_grad.shape[2]
    any_spec = pl.BlockSpec(memory_space=pl.ANY)
    V, D = pltpu.VMEM, pltpu.SemaphoreType.DMA
    return pl.pallas_call(
        kernel,
        out_shape=jax.ShapeDtypeStruct((16, 1024), F32),
        in_specs=[any_spec] * 7,
        out_specs=pl.BlockSpec(memory_space=pltpu.VMEM),
        scratch_shapes=[
            pltpu.SMEM((2,), jnp.int32),
            pltpu.SMEM((128,), jnp.int32),
            pltpu.SMEM((128,), jnp.int32),
            V((2, 128, ff), BF16),
            V((2, 128, d), BF16),
            V((4, TOK, ff), BF16),
            V((4, TOK, d), BF16),
            V((1024, 1024), BF16),
            V((2, 2, 128, 128), F32),
            V((2, 128, 128), F32),
            V((2, 128, 128), F32),
            V((2, 128, 128), F32),
            V((2, 128, 128), F32),
            V((64, 128), F32),
            V((2, 2, 8, 128), F32),
            V((2, 8, 128), F32),
            V((2, 8, 128), F32),
            V((128, 8, 128), F32),
            V((512, 128), F32),
            V((4, 16, 128), F32),
            V((3, 16, 128), F32),
            V((4, 4, 16, 256), F32),
            V((4, 3, 16, 256), F32),
            V((8, 128), F32),
            V((3, 8, 128), F32),
            V((1024, 128), F32),
            D((5,)),
            D((4,)),
            D((4,)),
            D((7,)),
            D((7,)),
            D((32,)),
            D((32,)),
            D((24,)),
            D((24,)),
            pltpu.SemaphoreType.REGULAR((NZ + 1,)),
            D((3,)),
            D((3,)),
            D((3,)),
            D((3,)),
            D((12,)),
            D((12,)),
        ],
        compiler_params=pltpu.CompilerParams(
            collective_id=0, has_side_effects=True, vmem_limit_bytes=60 * 1024 * 1024
        ),
    )(lengths, pair_perm, hidden, out_grad, proj_in, proj_out, bank_slab)


def solution(mesh):
    return jax.shard_map(
        per_device,
        mesh=mesh,
        in_specs=(
            P("bank", None, "tp"),
            P("bank", None, "tp"),
            P(None, "tp"),
            P(None, "tp"),
            P("bank"),
            P(),
            P("bank", "tp"),
        ),
        out_specs=P("tp", "bank"),
        check_vma=False,
    )
```

```python
import jax
import jax.numpy as jnp
from jax import lax
from jax.experimental import pallas as pl
from jax.experimental.pallas import tpu as pltpu
from jax.sharding import PartitionSpec as P

EPS = 1e-06
MESH = pl.DeviceIdType.MESH
F32, BF16 = jnp.float32, jnp.bfloat16
NX, NY, NZ = 4, 4, 8
TOK = 256
HI = lax.Precision.HIGHEST
NT = (((1,), (1,)), ((), ()))
EARLY, LATE = (0, 1, 2, 3), (7, 4, 6, 5)
GROUPS = (0, 1, 2, 3, 7, 6, 5, 4)


def kernel(
    len_hbm, perm_hbm, hid, og, pin, pout, bank, out_ref,
    len_s, perm_s, slot_s, win, wout, hbuf, obuf, bbuf, part, total, ra, rc, rx,
    gsc, tbuf, r4, tsum, gb, qf, qsb, qr, dbuf, dr, btile, br, sqb,
    ld_sem, h_sem, o_sem, x_ss, x_rs, g_ss, g_rs, y_ss, y_rs, ready,
    b_ss, b_rs, q_ss, q_rs, d_ss, d_rs,
):
    b, k = lax.axis_index("bank"), lax.axis_index("tp")
    xh, z, y = b // (NZ * NY), (b // NY) % NZ, b % NY
    xl, c = k // 2, k % 2
    x = xh * 2 + xl

    def dev(xx, yy, zz, cc):
        return ((xx // 2) * (NZ * NY) + zz * NY + yy, (xx % 2) * 2 + cc)

    tp_of = {1: xl * 2 + 1 - c, 2: (1 - xl) * 2 + c, 3: (1 - xl) * 2 + 1 - c}

    owners = ((1 - xl, c), (1 - xl, 1 - c), (xl, 1 - c), (xl, c))

    def load(src, dst, sem):
        cp = pltpu.make_async_copy(src, dst, sem)
        cp.start()
        return cp

    def block(s):
        xo, co = owners[s]
        return xo, pl.ds(pl.multiple_of(co * TOK, TOK), TOK)

    def load_og(s):
        return load(og.at[block(s)], obuf.at[s], o_sem.at[s])

    def load_hid(s):
        return load(hid.at[block(s)], hbuf.at[s], h_sem.at[s])

    cp_pout = load(pout, wout.at[0, pl.ds(0, 64)], ld_sem.at[1])
    ogs = [load_og(0), load_og(1)]
    cp_pin = load(pin, win.at[0, pl.ds(0, 64)], ld_sem.at[0])
    hids = [load_hid(0), load_hid(1)]

    barrier = pltpu.get_barrier_semaphore()

    def greet(sem, to):
        pl.semaphore_signal(sem, inc=1, device_id=to, device_id_type=MESH)

    for r in (1, 2, 3):
        greet(barrier, (b, tp_of[r]))
    for zz in range(NZ):
        for xx in range(NX):

            @pl.when(jnp.logical_or(zz > z, jnp.logical_and(zz == z, xx // 2 > xh)))
            def _(zz=zz, xx=xx):
                greet(barrier, dev(xx, y, zz, c))

    for yy in range(1, NY):

        @pl.when(yy > y)
        def _(yy=yy):
            greet(barrier, dev(x, yy, z, c))

    def greet_back():
        for zz in range(NZ):

            @pl.when(jnp.logical_and(xh == 1, jnp.logical_or(zz < z, jnp.logical_and(zz == z, xl == 0))))
            def _(zz=zz):
                for dx in range(2):
                    greet(ready.at[z], dev(2 * xl + dx, y, zz, c))

        for yy in range(NY - 1):

            @pl.when(yy < y)
            def _(yy=yy):
                greet(ready.at[NZ], dev(x, yy, z, c))

    for w in (win, wout):
        w[0, pl.ds(64, 64)] = jnp.zeros((64, w.shape[2]), BF16)
        w[1, pl.ds(0, 64)] = jnp.zeros((64, w.shape[2]), BF16)

    def send(src, dst, ss, rs, to):
        cp = pltpu.make_async_remote_copy(
            src_ref=src, dst_ref=dst, send_sem=ss, recv_sem=rs, device_id=to, device_id_type=MESH
        )
        cp.start()
        return cp

    sent = []

    def packed(rows, s, w):
        low = lax.dot_general(rows[s, pl.ds(0, 128)], w[0], NT, preferred_element_type=F32)
        return low + lax.dot_general(rows[s, pl.ds(128, 128)], w[1], NT, preferred_element_type=F32)

    pair, cross = (b, tp_of[1]), (b, tp_of[3])
    cp_pout.wait()
    wout[1, pl.ds(64, 64)] = wout[0, pl.ds(0, 64)]
    ogs[0].wait()
    ogs += [load_og(2), load_og(3)]
    hids.append(load_hid(2))
    part[0, 0] = packed(obuf, 0, wout)
    pl.semaphore_wait(barrier, 3 + NX * z + 2 * xh + y)
    greet_back()
    ca = [send(part.at[0, 0], ra.at[0], x_ss.at[0], x_rs.at[0], pair)]
    ogs[1].wait()
    out_b = packed(obuf, 1, wout)
    cp_pin.wait()
    win[1, pl.ds(64, 64)] = win[0, pl.ds(0, 64)]
    hids[0].wait()
    hids.append(load_hid(3))
    part[0, 1] = packed(hbuf, 0, win)
    ca.append(send(part.at[0, 1], ra.at[1], x_ss.at[1], x_rs.at[1], pair))
    ca[0].wait_recv()
    total[0] = out_b + ra[0]
    cx = [send(total.at[0], rx.at[0], x_ss.at[2], x_rs.at[2], cross)]
    hids[1].wait()
    in_b = packed(hbuf, 1, win)
    ca[1].wait_recv()
    total[1] = in_b + ra[1]
    cx.append(send(total.at[1], rx.at[1], x_ss.at[3], x_rs.at[3], cross))
    cp_len = load(len_hbm, len_s, ld_sem.at[2])
    cp_perm = load(perm_hbm, perm_s, ld_sem.at[3])
    cp_bank = load(bank, bbuf, ld_sem.at[4])
    ogs[2].wait()
    part[1, 0] = packed(obuf, 2, wout)
    cc = [send(part.at[1, 0], rc.at[0], x_ss.at[4], x_rs.at[4], pair)]
    hids[2].wait()
    part[1, 1] = packed(hbuf, 2, win)
    cc.append(send(part.at[1, 1], rc.at[1], x_ss.at[5], x_rs.at[5], pair))
    ogs[3].wait()
    out_d = packed(obuf, 3, wout)
    hids[3].wait()
    in_d = packed(hbuf, 3, win)
    cp_len.wait()
    cp_perm.wait()
    cc[0].wait_recv()
    cx[0].wait_recv()
    out_d = out_d + rc[0] + rx[0]
    cc[1].wait_recv()
    in_d = in_d + rc[1]
    cx[1].wait_recv()
    in_d = in_d + rx[1]
    sent += ca + cx + cc

    lane = lax.broadcasted_iota(jnp.int32, (128, 128), 1)
    pos = lax.broadcasted_iota(jnp.int32, (128, 128), 0) + jnp.where(lane < 64, 0, 128) + c * TOK
    live = jnp.where(pos < len_s[xl], in_d, 0.0)
    outer = jnp.dot(jnp.transpose(live), out_d, precision=HI, preferred_element_type=F32)
    halves = jnp.where(lane[0:64] < 64, outer[0:64], outer[64:128])
    gsc[...] = halves + pltpu.roll(halves, 64, axis=1)
    even, odd = gsc[pl.ds(0, 32, stride=2), :], gsc[pl.ds(1, 32, stride=2), :]
    tiles = jnp.where(lane[0:32] < 64, even, odd)
    for to_x in range(2):
        for to_c in range(2):
            share = to_x * 2 + to_c
            tbuf[to_c, to_x] = tiles[8 * share : 8 * share + 8]
    c4 = send(tbuf.at[1 - c], r4, x_ss.at[6], x_rs.at[6], pair)
    c4.wait_recv()
    sent.append(c4)
    tsum[...] = tbuf[c] + r4[...]
    mine = y * (NZ * NX) + z * NX + x
    gb[mine] = tsum[xl]

    def plane_copy(tx, tz, slot):
        return pltpu.make_async_remote_copy(
            src_ref=tsum.at[tx % 2], dst_ref=gb.at[mine], send_sem=g_ss.at[slot], recv_sem=g_rs.at[z * NX + x],
            device_id=dev(tx, y, tz, c), device_id_type=MESH,
        )

    def to_rows(rows):
        for tz in rows:

            @pl.when(jnp.logical_or(tz > z, jnp.logical_and(tz == z, xh == 0)))
            def _(tz=tz):
                pl.semaphore_wait(ready.at[tz], 1)

            for dx in (2, 1, 3):
                plane_copy((x + dx) % NX, tz, tz * NX + dx).start()

            @pl.when(tz != z)
            def _(tz=tz):
                plane_copy(x, tz, tz * NX).start()

    to_rows(EARLY)

    @pl.when(z >= 4)
    def _():
        to_rows(LATE)

    cp_bank.wait()

    def bank_rows(i, carry):
        rows = pl.ds(pl.multiple_of(i * 128, 128), 128)
        acc = jnp.zeros((128, 128), F32)
        for j in range(8):
            v = bbuf[rows, pl.ds(128 * j, 128)].astype(F32)
            acc = acc + v * v
        sqb[rows, :] = acc
        return carry

    lax.fori_loop(0, 8, bank_rows, 0)
    sums = lax.dot_general(jnp.ones((8, 128), F32), sqb[...], NT, precision=HI, preferred_element_type=F32)
    sub = lax.broadcasted_iota(jnp.int32, (8, 128), 0)
    tile = jnp.zeros((8, 128), F32)
    for j in range(8):
        tile = jnp.where(sub == j, sums[:, 128 * j : 128 * j + 128], tile)
    btile[...] = tile
    bcp = {r: send(btile, br.at[r - 1], b_ss.at[r - 1], b_rs.at[r - 1], (b, tp_of[r])) for r in (1, 2, 3)}

    def slots(i, carry):
        e = perm_s[i]
        slot_s[i] = ((e // 2) % 4) * (NZ * NX) + ((e // 8) % 8) * NX + (e // 64) * 2 + e % 2
        return carry

    lax.fori_loop(0, 128, slots, 0)

    up, down = dev(x, (y + 1) % NY, z, c), dev(x, (y + NY - 1) % NY, z, c)

    def group(yy, zz):
        return gb.at[pl.ds(((yy + NY) % NY) * (NZ * NX) + zz * NX, NX)]

    def plane_wait(zz, xx):
        pltpu.make_async_remote_copy(
            src_ref=tsum.at[0], dst_ref=gb.at[mine], send_sem=g_ss.at[0], recv_sem=g_rs.at[zz * NX + xx],
            device_id=up, device_id_type=MESH,
        ).wait_recv()

    across = dev(x, (y + 2) % NY, z, c)
    along = []

    @pl.when(y < NY - 1)
    def _():
        pl.semaphore_wait(ready.at[NZ], NY - 1 - y)

    for i, zz in enumerate(GROUPS):
        if i == 1:

            @pl.when(z < 4)
            def _():
                to_rows(LATE)

        for xx in range(NX):

            @pl.when(jnp.logical_or(zz != z, xx != x))
            def _(zz=zz, xx=xx):
                plane_wait(zz, xx)

        for n, to in enumerate((across, up, down)):
            slot = n * NZ + zz
            along.append(send(group(y, zz), group(y, zz), y_ss.at[slot], y_rs.at[slot], to))
    for cp in along:
        cp.wait_recv()
    sent += along

    def query(p, carry):
        rows = pl.ds(pl.multiple_of(p * 8, 8), 8)
        qf[rows, :] = gb[slot_s[2 * p + 1]] - gb[slot_s[2 * p]]
        return carry

    lax.fori_loop(0, 64, query, 0, unroll=8)
    cols, acc = [], jnp.zeros((64, 128), F32)
    for v in range(8):
        part = qf[pl.ds(v, 64, stride=8), :]
        acc = acc + part * part
        cols.append(part.astype(BF16))
    low = jnp.concatenate(cols, axis=1)
    qsq = jnp.broadcast_to(jnp.sum(acc, axis=1, keepdims=True), (64, 128))
    for s in range(4):
        qsb[s] = qsq[16 * s : 16 * s + 16]
    dcp = {}
    for j in range(4):
        part = lax.dot_general(low, bbuf[pl.ds(256 * j, 256), :], NT, preferred_element_type=F32)
        for s in range(4):
            dbuf[j, s] = part[16 * s : 16 * s + 16]
        for r in (2, 3, 1):
            dcp[j, r] = send(
                dbuf.at[j, tp_of[r]], dr.at[j, r - 1], d_ss.at[j * 3 + r - 1], d_rs.at[j * 3 + r - 1], (b, tp_of[r])
            )
    qcp = {r: send(qsb.at[tp_of[r]], qr.at[r - 1], q_ss.at[r - 1], q_rs.at[r - 1], (b, tp_of[r])) for r in (2, 3, 1)}
    for r in (1, 2, 3):
        bcp[r].wait_recv()
    norms = lax.rsqrt(btile[...] + br[0] + br[1] + br[2] + EPS)
    for r in (1, 2, 3):
        qcp[r].wait_recv()
    scale = lax.rsqrt(qsb[k] + qr[0] + qr[1] + qr[2] + EPS) * 64.0
    for j in range(4):
        for r in (1, 2, 3):
            dcp[j, r].wait_recv()
        for h in range(2):
            cs = pl.ds(128 * h, 128)
            total = dbuf[j, k, :, cs] + dr[j, 0, :, cs] + dr[j, 1, :, cs] + dr[j, 2, :, cs]
            n = 2 * j + h
            out_ref[:, pl.ds(128 * n, 128)] = total * scale * norms[n : n + 1, :]
    sent += list(bcp.values()) + list(qcp.values()) + list(dcp.values())
    for cp in sent:
        cp.wait_send()
    for tz in EARLY + LATE:
        for dx in (2, 1, 3):
            plane_copy((x + dx) % NX, tz, tz * NX + dx).wait_send()

        @pl.when(tz != z)
        def _(tz=tz):
            plane_copy(x, tz, tz * NX).wait_send()


def per_device(hidden, out_grad, proj_in, proj_out, lengths, pair_perm, bank_slab):
    ff, d = hidden.shape[2], out_grad.shape[2]
    any_spec = pl.BlockSpec(memory_space=pl.ANY)
    V, D = pltpu.VMEM, pltpu.SemaphoreType.DMA
    return pl.pallas_call(
        kernel,
        out_shape=jax.ShapeDtypeStruct((16, 1024), F32),
        in_specs=[any_spec] * 7,
        out_specs=pl.BlockSpec(memory_space=pltpu.VMEM),
        scratch_shapes=[
            pltpu.SMEM((2,), jnp.int32),
            pltpu.SMEM((128,), jnp.int32),
            pltpu.SMEM((128,), jnp.int32),
            V((2, 128, ff), BF16),
            V((2, 128, d), BF16),
            V((4, TOK, ff), BF16),
            V((4, TOK, d), BF16),
            V((1024, 1024), BF16),
            V((2, 2, 128, 128), F32),
            V((2, 128, 128), F32),
            V((2, 128, 128), F32),
            V((2, 128, 128), F32),
            V((2, 128, 128), F32),
            V((64, 128), F32),
            V((2, 2, 8, 128), F32),
            V((2, 8, 128), F32),
            V((2, 8, 128), F32),
            V((128, 8, 128), F32),
            V((512, 128), F32),
            V((4, 16, 128), F32),
            V((3, 16, 128), F32),
            V((4, 4, 16, 256), F32),
            V((4, 3, 16, 256), F32),
            V((8, 128), F32),
            V((3, 8, 128), F32),
            V((1024, 128), F32),
            D((5,)),
            D((4,)),
            D((4,)),
            D((7,)),
            D((7,)),
            D((32,)),
            D((32,)),
            D((24,)),
            D((24,)),
            pltpu.SemaphoreType.REGULAR((NZ + 1,)),
            D((3,)),
            D((3,)),
            D((3,)),
            D((3,)),
            D((12,)),
            D((12,)),
        ],
        compiler_params=pltpu.CompilerParams(
            collective_id=0, has_side_effects=True, vmem_limit_bytes=60 * 1024 * 1024
        ),
    )(lengths, pair_perm, hidden, out_grad, proj_in, proj_out, bank_slab)


def solution(mesh):
    return jax.shard_map(
        per_device,
        mesh=mesh,
        in_specs=(
            P("bank", None, "tp"),
            P("bank", None, "tp"),
            P(None, "tp"),
            P(None, "tp"),
            P("bank"),
            P(),
            P("bank", "tp"),
        ),
        out_specs=P("tp", "bank"),
        check_vma=False,
    )
```

```python
import jax
import jax.numpy as jnp
from jax import lax
from jax.experimental import pallas as pl
from jax.experimental.pallas import tpu as pltpu
from jax.sharding import PartitionSpec as P

EPS = 1e-06
MESH = pl.DeviceIdType.MESH
F32, BF16 = jnp.float32, jnp.bfloat16
NX, NY, NZ = 4, 4, 8
TOK = 256
HI = lax.Precision.HIGHEST
NT = (((1,), (1,)), ((), ()))
EARLY, LATE = (0, 1, 2, 3), (7, 4, 6, 5)
GROUPS = (0, 1, 2, 3, 7, 6, 5, 4)


def kernel(
    len_hbm, perm_hbm, hid, og, pin, pout, bank, out_ref,
    len_s, perm_s, slot_s, win, wout, hbuf, obuf, bbuf, part, total, ra, rc, rx,
    gsc, tbuf, r4, tsum, gb, qf, qsb, qr, dbuf, dr, btile, br, sqb,
    ld_sem, h_sem, o_sem, x_ss, x_rs, g_ss, g_rs, y_ss, y_rs, ready,
    b_ss, b_rs, q_ss, q_rs, d_ss, d_rs,
):
    b, k = lax.axis_index("bank"), lax.axis_index("tp")
    xh, z, y = b // (NZ * NY), (b // NY) % NZ, b % NY
    xl, c = k // 2, k % 2
    x = xh * 2 + xl

    def dev(xx, yy, zz, cc):
        return ((xx // 2) * (NZ * NY) + zz * NY + yy, (xx % 2) * 2 + cc)

    tp_of = {1: xl * 2 + 1 - c, 2: (1 - xl) * 2 + c, 3: (1 - xl) * 2 + 1 - c}

    owners = ((1 - xl, c), (1 - xl, 1 - c), (xl, 1 - c), (xl, c))

    def load(src, dst, sem):
        cp = pltpu.make_async_copy(src, dst, sem)
        cp.start()
        return cp

    def block(s):
        xo, co = owners[s]
        return xo, pl.ds(pl.multiple_of(co * TOK, TOK), TOK)

    def load_og(s):
        return load(og.at[block(s)], obuf.at[s], o_sem.at[s])

    def load_hid(s):
        return load(hid.at[block(s)], hbuf.at[s], h_sem.at[s])

    cp_pout = load(pout, wout.at[0, pl.ds(0, 64)], ld_sem.at[1])
    ogs = [load_og(0), load_og(1)]
    cp_pin = load(pin, win.at[0, pl.ds(0, 64)], ld_sem.at[0])
    hids = [load_hid(0)]

    barrier = pltpu.get_barrier_semaphore()

    def greet(sem, to):
        pl.semaphore_signal(sem, inc=1, device_id=to, device_id_type=MESH)

    for r in (1, 2, 3):
        greet(barrier, (b, tp_of[r]))
    for zz in range(NZ):
        for xx in range(NX):

            @pl.when(jnp.logical_or(zz > z, jnp.logical_and(zz == z, xx // 2 > xh)))
            def _(zz=zz, xx=xx):
                greet(barrier, dev(xx, y, zz, c))

    for yy in range(1, NY):

        @pl.when(yy > y)
        def _(yy=yy):
            greet(barrier, dev(x, yy, z, c))

    def greet_back():
        for zz in range(NZ):

            @pl.when(jnp.logical_and(xh == 1, jnp.logical_or(zz < z, jnp.logical_and(zz == z, xl == 0))))
            def _(zz=zz):
                for dx in range(2):
                    greet(ready.at[z], dev(2 * xl + dx, y, zz, c))

        for yy in range(NY - 1):

            @pl.when(yy < y)
            def _(yy=yy):
                greet(ready.at[NZ], dev(x, yy, z, c))

    for w in (win, wout):
        w[0, pl.ds(64, 64)] = jnp.zeros((64, w.shape[2]), BF16)
        w[1, pl.ds(0, 64)] = jnp.zeros((64, w.shape[2]), BF16)

    def send(src, dst, ss, rs, to):
        cp = pltpu.make_async_remote_copy(
            src_ref=src, dst_ref=dst, send_sem=ss, recv_sem=rs, device_id=to, device_id_type=MESH
        )
        cp.start()
        return cp

    sent = []

    def packed(rows, s, w):
        low = lax.dot_general(rows[s, pl.ds(0, 128)], w[0], NT, preferred_element_type=F32)
        return low + lax.dot_general(rows[s, pl.ds(128, 128)], w[1], NT, preferred_element_type=F32)

    pair, cross = (b, tp_of[1]), (b, tp_of[3])
    cp_pout.wait()
    wout[1, pl.ds(64, 64)] = wout[0, pl.ds(0, 64)]
    ogs[0].wait()
    hids.append(load_hid(1))
    part[0, 0] = packed(obuf, 0, wout)
    pl.semaphore_wait(barrier, 3 + NX * z + 2 * xh + y)
    greet_back()
    ca = [send(part.at[0, 0], ra.at[0], x_ss.at[0], x_rs.at[0], pair)]
    ogs[1].wait()
    out_b = packed(obuf, 1, wout)
    cp_pin.wait()
    win[1, pl.ds(64, 64)] = win[0, pl.ds(0, 64)]
    hids[0].wait()
    ogs += [load_og(2), load_og(3)]
    hids.append(load_hid(2))
    part[0, 1] = packed(hbuf, 0, win)
    ca.append(send(part.at[0, 1], ra.at[1], x_ss.at[1], x_rs.at[1], pair))
    ca[0].wait_recv()
    total[0] = out_b + ra[0]
    cx = [send(total.at[0], rx.at[0], x_ss.at[2], x_rs.at[2], cross)]
    hids[1].wait()
    hids.append(load_hid(3))
    in_b = packed(hbuf, 1, win)
    ca[1].wait_recv()
    total[1] = in_b + ra[1]
    cx.append(send(total.at[1], rx.at[1], x_ss.at[3], x_rs.at[3], cross))
    cp_len = load(len_hbm, len_s, ld_sem.at[2])
    cp_perm = load(perm_hbm, perm_s, ld_sem.at[3])
    cp_bank = load(bank, bbuf, ld_sem.at[4])
    ogs[2].wait()
    part[1, 0] = packed(obuf, 2, wout)
    cc = [send(part.at[1, 0], rc.at[0], x_ss.at[4], x_rs.at[4], pair)]
    hids[2].wait()
    part[1, 1] = packed(hbuf, 2, win)
    cc.append(send(part.at[1, 1], rc.at[1], x_ss.at[5], x_rs.at[5], pair))
    ogs[3].wait()
    out_d = packed(obuf, 3, wout)
    hids[3].wait()
    in_d = packed(hbuf, 3, win)
    cp_len.wait()
    cp_perm.wait()
    cc[0].wait_recv()
    cx[0].wait_recv()
    out_d = out_d + rc[0] + rx[0]
    cc[1].wait_recv()
    in_d = in_d + rc[1]
    cx[1].wait_recv()
    in_d = in_d + rx[1]
    sent += ca + cx + cc

    lane = lax.broadcasted_iota(jnp.int32, (128, 128), 1)
    pos = lax.broadcasted_iota(jnp.int32, (128, 128), 0) + jnp.where(lane < 64, 0, 128) + c * TOK
    live = jnp.where(pos < len_s[xl], in_d, 0.0)
    outer = jnp.dot(jnp.transpose(live), out_d, precision=HI, preferred_element_type=F32)
    halves = jnp.where(lane[0:64] < 64, outer[0:64], outer[64:128])
    gsc[...] = halves + pltpu.roll(halves, 64, axis=1)
    even, odd = gsc[pl.ds(0, 32, stride=2), :], gsc[pl.ds(1, 32, stride=2), :]
    tiles = jnp.where(lane[0:32] < 64, even, odd)
    for to_x in range(2):
        for to_c in range(2):
            share = to_x * 2 + to_c
            tbuf[to_c, to_x] = tiles[8 * share : 8 * share + 8]
    c4 = send(tbuf.at[1 - c], r4, x_ss.at[6], x_rs.at[6], pair)
    c4.wait_recv()
    sent.append(c4)
    tsum[...] = tbuf[c] + r4[...]
    mine = y * (NZ * NX) + z * NX + x
    gb[mine] = tsum[xl]

    def plane_copy(tx, tz, slot):
        return pltpu.make_async_remote_copy(
            src_ref=tsum.at[tx % 2], dst_ref=gb.at[mine], send_sem=g_ss.at[slot], recv_sem=g_rs.at[z * NX + x],
            device_id=dev(tx, y, tz, c), device_id_type=MESH,
        )

    def to_rows(rows):
        for tz in rows:

            @pl.when(jnp.logical_or(tz > z, jnp.logical_and(tz == z, xh == 0)))
            def _(tz=tz):
                pl.semaphore_wait(ready.at[tz], 1)

            for dx in (2, 1, 3):
                plane_copy((x + dx) % NX, tz, tz * NX + dx).start()

            @pl.when(tz != z)
            def _(tz=tz):
                plane_copy(x, tz, tz * NX).start()

    to_rows(EARLY)

    @pl.when(z >= 4)
    def _():
        to_rows(LATE)

    cp_bank.wait()

    def bank_rows(i, carry):
        rows = pl.ds(pl.multiple_of(i * 128, 128), 128)
        acc = jnp.zeros((128, 128), F32)
        for j in range(8):
            v = bbuf[rows, pl.ds(128 * j, 128)].astype(F32)
            acc = acc + v * v
        sqb[rows, :] = acc
        return carry

    lax.fori_loop(0, 8, bank_rows, 0)
    sums = lax.dot_general(jnp.ones((8, 128), F32), sqb[...], NT, precision=HI, preferred_element_type=F32)
    sub = lax.broadcasted_iota(jnp.int32, (8, 128), 0)
    tile = jnp.zeros((8, 128), F32)
    for j in range(8):
        tile = jnp.where(sub == j, sums[:, 128 * j : 128 * j + 128], tile)
    btile[...] = tile
    bcp = {r: send(btile, br.at[r - 1], b_ss.at[r - 1], b_rs.at[r - 1], (b, tp_of[r])) for r in (1, 2, 3)}

    def slots(i, carry):
        e = perm_s[i]
        slot_s[i] = ((e // 2) % 4) * (NZ * NX) + ((e // 8) % 8) * NX + (e // 64) * 2 + e % 2
        return carry

    lax.fori_loop(0, 128, slots, 0)

    up, down = dev(x, (y + 1) % NY, z, c), dev(x, (y + NY - 1) % NY, z, c)

    def group(yy, zz):
        return gb.at[pl.ds(((yy + NY) % NY) * (NZ * NX) + zz * NX, NX)]

    def plane_wait(zz, xx):
        pltpu.make_async_remote_copy(
            src_ref=tsum.at[0], dst_ref=gb.at[mine], send_sem=g_ss.at[0], recv_sem=g_rs.at[zz * NX + xx],
            device_id=up, device_id_type=MESH,
        ).wait_recv()

    across = dev(x, (y + 2) % NY, z, c)
    along = []

    @pl.when(y < NY - 1)
    def _():
        pl.semaphore_wait(ready.at[NZ], NY - 1 - y)

    for i, zz in enumerate(GROUPS):
        if i == 1:

            @pl.when(z < 4)
            def _():
                to_rows(LATE)

        for xx in range(NX):

            @pl.when(jnp.logical_or(zz != z, xx != x))
            def _(zz=zz, xx=xx):
                plane_wait(zz, xx)

        for n, to in enumerate((across, up, down)):
            slot = n * NZ + zz
            along.append(send(group(y, zz), group(y, zz), y_ss.at[slot], y_rs.at[slot], to))
    for cp in along:
        cp.wait_recv()
    sent += along

    def query(p, carry):
        rows = pl.ds(pl.multiple_of(p * 8, 8), 8)
        qf[rows, :] = gb[slot_s[2 * p + 1]] - gb[slot_s[2 * p]]
        return carry

    lax.fori_loop(0, 64, query, 0, unroll=8)
    cols, acc = [], jnp.zeros((64, 128), F32)
    for v in range(8):
        part = qf[pl.ds(v, 64, stride=8), :]
        acc = acc + part * part
        cols.append(part.astype(BF16))
    low = jnp.concatenate(cols, axis=1)
    qsq = jnp.broadcast_to(jnp.sum(acc, axis=1, keepdims=True), (64, 128))
    for s in range(4):
        qsb[s] = qsq[16 * s : 16 * s + 16]
    qcp = {r: send(qsb.at[tp_of[r]], qr.at[r - 1], q_ss.at[r - 1], q_rs.at[r - 1], (b, tp_of[r])) for r in (2, 3, 1)}
    dcp = {}
    for j in range(8):
        part = lax.dot_general(low, bbuf[pl.ds(128 * j, 128), :], NT, preferred_element_type=F32)
        for s in range(4):
            dbuf[j, s] = part[16 * s : 16 * s + 16]
        for r in (2, 3, 1):
            dcp[j, r] = send(
                dbuf.at[j, tp_of[r]], dr.at[j, r - 1], d_ss.at[j * 3 + r - 1], d_rs.at[j * 3 + r - 1], (b, tp_of[r])
            )
    for r in (1, 2, 3):
        bcp[r].wait_recv()
    norms = lax.rsqrt(btile[...] + br[0] + br[1] + br[2] + EPS)
    for r in (1, 2, 3):
        qcp[r].wait_recv()
    scale = lax.rsqrt(qsb[k] + qr[0] + qr[1] + qr[2] + EPS) * 64.0
    for j in range(8):
        for r in (1, 2, 3):
            dcp[j, r].wait_recv()
        dots = dbuf[j, k] + dr[j, 0] + dr[j, 1] + dr[j, 2]
        out_ref[:, pl.ds(128 * j, 128)] = dots * scale * norms[j : j + 1, :]
    sent += list(bcp.values()) + list(qcp.values()) + list(dcp.values())
    for cp in sent:
        cp.wait_send()
    for tz in EARLY + LATE:
        for dx in (2, 1, 3):
            plane_copy((x + dx) % NX, tz, tz * NX + dx).wait_send()

        @pl.when(tz != z)
        def _(tz=tz):
            plane_copy(x, tz, tz * NX).wait_send()


def per_device(hidden, out_grad, proj_in, proj_out, lengths, pair_perm, bank_slab):
    ff, d = hidden.shape[2], out_grad.shape[2]
    any_spec = pl.BlockSpec(memory_space=pl.ANY)
    V, D = pltpu.VMEM, pltpu.SemaphoreType.DMA
    return pl.pallas_call(
        kernel,
        out_shape=jax.ShapeDtypeStruct((16, 1024), F32),
        in_specs=[any_spec] * 7,
        out_specs=pl.BlockSpec(memory_space=pltpu.VMEM),
        scratch_shapes=[
            pltpu.SMEM((2,), jnp.int32),
            pltpu.SMEM((128,), jnp.int32),
            pltpu.SMEM((128,), jnp.int32),
            V((2, 128, ff), BF16),
            V((2, 128, d), BF16),
            V((4, TOK, ff), BF16),
            V((4, TOK, d), BF16),
            V((1024, 1024), BF16),
            V((2, 2, 128, 128), F32),
            V((2, 128, 128), F32),
            V((2, 128, 128), F32),
            V((2, 128, 128), F32),
            V((2, 128, 128), F32),
            V((64, 128), F32),
            V((2, 2, 8, 128), F32),
            V((2, 8, 128), F32),
            V((2, 8, 128), F32),
            V((128, 8, 128), F32),
            V((512, 128), F32),
            V((4, 16, 128), F32),
            V((3, 16, 128), F32),
            V((8, 4, 16, 128), F32),
            V((8, 3, 16, 128), F32),
            V((8, 128), F32),
            V((3, 8, 128), F32),
            V((1024, 128), F32),
            D((5,)),
            D((4,)),
            D((4,)),
            D((7,)),
            D((7,)),
            D((32,)),
            D((32,)),
            D((24,)),
            D((24,)),
            pltpu.SemaphoreType.REGULAR((NZ + 1,)),
            D((3,)),
            D((3,)),
            D((3,)),
            D((3,)),
            D((24,)),
            D((24,)),
        ],
        compiler_params=pltpu.CompilerParams(
            collective_id=0, has_side_effects=True, vmem_limit_bytes=60 * 1024 * 1024
        ),
    )(lengths, pair_perm, hidden, out_grad, proj_in, proj_out, bank_slab)


def solution(mesh):
    return jax.shard_map(
        per_device,
        mesh=mesh,
        in_specs=(
            P("bank", None, "tp"),
            P("bank", None, "tp"),
            P(None, "tp"),
            P(None, "tp"),
            P("bank"),
            P(),
            P("bank", "tp"),
        ),
        out_specs=P("tp", "bank"),
        check_vma=False,
    )
```
